32 devices in a mesh: rows: 4 (over y, x), cols: 8 (over z, core).
Axes of the slice: x: 2, y: 2, z: 4, core: 2. Of those that a mesh axis runs over, the one named last changes fastest.
Arguments:
- object_tiles: float32 [2, 2, 3072, 6144], P(None, None, 'rows', 'cols'), may hold values from -6 to 6
- probe: float32 [2, 512, 512], replicated, may hold values from -6 to 6
- prop_phase: float32 [512, 512], replicated, may hold values from -3.140625 to 3.140625
- amplitudes: bfloat16 [4, 8, 1, 512, 512], P('rows', 'cols'), may hold values from 0 to 2
- offsets: int32 [4, 8, 1, 2], P('rows', 'cols'), may hold values from 0 to 512
- counts: int32 [4, 8], P('rows', 'cols'), may hold values from 0 to 1
- step_size: float32 [2], replicated, may hold values from 0.3 to 1
Outputs:
- updated: float32 [2, 2, 3072, 6144], P(None, None, 'rows', 'cols')
The draws below stay inside these ranges and needn't reach their ends.
Inputs may be any that keep to these rules, and one draw needn't show every extreme that they name: `offsets`: row and column of a window's first cell in the device's tile extended by 128 cells on every side. `counts`: slots at or past a tile's count are ignored; a tile may have no probe position.
All inputs are finite; a program needn't handle non-finite values.
Results may differ from the reference program's by a relative error of at most 0.013.
The reference program's roundings to bfloat16 on the way count: a program that leaves them out, or rounds other values in their place, can miss the bound.
Values sent between devices are 32-bit elements; how exact they have to be, the bound alone decides.
A program may use at most 192 MiB of HBM per device.

```python
import math
import jax
import jax.numpy as jnp
from jax import lax

P_SIZE = 512
H = 128
TILE = 768
MAXP = 1
TROWS = 4
TCOLS = 8
NR = 3072
NC = 6144


def with_ends(entries, own_key, smallest, largest):
    extent = entries.shape
    place = [jax.random.randint(jax.random.fold_in(own_key, axis), (), 0, extent[axis]) for axis in range(len(extent))]
    entries = entries.at[tuple(place)].set(smallest)
    longest = extent.index(max(extent))
    place[longest] = (place[longest] + 1) % extent[longest]
    return entries.at[tuple(place)].set(largest)


def block_scale(stream_key, shape, cuts, least, top_value):
    loudness, own = 1.0, jax.random.fold_in(stream_key, 6)
    for dim, shards_of in cuts:
        draws = jnp.exp(jax.random.uniform(jax.random.fold_in(own, dim), (shards_of,), jnp.float32, least / len(cuts), top_value / len(cuts)))
        loudness = loudness * jnp.repeat(draws, shape[dim] // shards_of).reshape([-1 if axis == dim else 1 for axis in range(len(shape))])
    return loudness


def scatter_about(stream_key, dims, spread, reach, shards=(), kind=jnp.bfloat16):
    loudness = block_scale(stream_key, dims, shards, -0.22, 0.18) if shards else 1.0
    entries = jax.random.normal(stream_key, dims, jnp.float32) * spread * loudness
    return jnp.minimum(jnp.maximum(entries, -reach), reach).astype(kind)


def setup_inputs(seed: int = 0) -> dict:
    streams_of = jax.random.split(jax.random.key(seed), 8)
    object_tiles = scatter_about(streams_of[0], (2, 2, NR, NC), 1.0, 6.0, ((2, 4), (3, 8)), jnp.float32)
    probe = scatter_about(streams_of[1], (2, P_SIZE, P_SIZE), 1.0, 6.0, (), jnp.float32)
    prop_phase = jnp.clip(jax.random.uniform(streams_of[2], (P_SIZE, P_SIZE), jnp.float32, -3.140625, 3.140625), -3.140625, 3.140625)
    amplitudes = jnp.clip(2.0 * jax.random.uniform(streams_of[3], (TROWS, TCOLS, MAXP, P_SIZE, P_SIZE), jnp.float32) ** block_scale(streams_of[3], (TROWS, TCOLS, MAXP, P_SIZE, P_SIZE), ((0, 4), (1, 8)), -0.2, 0.2), 0.0, 2.0).astype(jnp.bfloat16)
    offsets = with_ends(jax.random.randint(streams_of[4], (TROWS, TCOLS, MAXP, 2), 0, TILE + 2 * H - P_SIZE + 1), jax.random.fold_in(streams_of[4], 1), 0, TILE + 2 * H - P_SIZE).astype(jnp.int32)
    counts = with_ends(jax.random.randint(streams_of[5], (TROWS, TCOLS), 0, MAXP + 1), jax.random.fold_in(streams_of[5], 1), 0, MAXP).astype(jnp.int32)
    step_size = jnp.clip(jnp.exp(jax.random.uniform(streams_of[6], (2,), jnp.float32, math.log(0.3), math.log(1.0))), 0.3, 1.0)
    return {"object_tiles": object_tiles, "probe": probe, "prop_phase": prop_phase, "amplitudes": amplitudes, "offsets": offsets, "counts": counts, "step_size": step_size}


def dft_tables(length, inverse):
    index = jnp.arange(length, dtype=jnp.int32)
    product = index[:, None] * index[None, :] % length
    angles = product.astype(jnp.float32) * (2.0 * math.pi / length)
    scaling = 1.0 / math.sqrt(length)
    direction = 1.0 if inverse else -1.0
    return ((jnp.cos(angles) * scaling).astype(jnp.bfloat16), (direction * jnp.sin(angles) * scaling).astype(jnp.bfloat16))

def transform(real_part, imag_part, tables):
    table_re, table_im = tables
    left_re = real_part.astype(jnp.bfloat16)
    left_im = imag_part.astype(jnp.bfloat16)
    mid_re = jnp.dot(table_re, left_re, preferred_element_type=jnp.float32) - jnp.dot(table_im, left_im, preferred_element_type=jnp.float32)
    mid_im = jnp.dot(table_re, left_im, preferred_element_type=jnp.float32) + jnp.dot(table_im, left_re, preferred_element_type=jnp.float32)
    mid_re = mid_re.astype(jnp.bfloat16)
    mid_im = mid_im.astype(jnp.bfloat16)
    out_re = jnp.dot(mid_re, table_re, preferred_element_type=jnp.float32) - jnp.dot(mid_im, table_im, preferred_element_type=jnp.float32)
    out_im = jnp.dot(mid_re, table_im, preferred_element_type=jnp.float32) + jnp.dot(mid_im, table_re, preferred_element_type=jnp.float32)
    return (out_re, out_im)

def probe_gradient(window, probe, kernel_re, kernel_im, measured, forward, backward):
    first_re, first_im = (window[0, 0], window[0, 1])
    second_re, second_im = (window[1, 0], window[1, 1])
    probe_re, probe_im = (probe[0], probe[1])
    wave_re = probe_re * first_re - probe_im * first_im
    wave_im = probe_re * first_im + probe_im * first_re
    spec_re, spec_im = transform(wave_re, wave_im, forward)
    prop_re = spec_re * kernel_re - spec_im * kernel_im
    prop_im = spec_re * kernel_im + spec_im * kernel_re
    psi1_re, psi1_im = transform(prop_re, prop_im, backward)
    exit_re = psi1_re * second_re - psi1_im * second_im
    exit_im = psi1_re * second_im + psi1_im * second_re
    far_re, far_im = transform(exit_re, exit_im, forward)
    magnitude = jnp.sqrt(far_re * far_re + far_im * far_im + 1.0)
    factor = 1.0 - measured.astype(jnp.float32) / magnitude
    chi2_re, chi2_im = transform(far_re * factor, far_im * factor, backward)
    grad2_re = psi1_re * chi2_re + psi1_im * chi2_im
    grad2_im = psi1_re * chi2_im - psi1_im * chi2_re
    back_re = second_re * chi2_re + second_im * chi2_im
    back_im = second_re * chi2_im - second_im * chi2_re
    bspec_re, bspec_im = transform(back_re, back_im, forward)
    bprop_re = bspec_re * kernel_re + bspec_im * kernel_im
    bprop_im = bspec_im * kernel_re - bspec_re * kernel_im
    dwave_re, dwave_im = transform(bprop_re, bprop_im, backward)
    grad1_re = probe_re * dwave_re + probe_im * dwave_im
    grad1_im = probe_re * dwave_im - probe_im * dwave_re
    return jnp.stack([jnp.stack([grad1_re, grad1_im]), jnp.stack([grad2_re, grad2_im])])

def reference(object_tiles, probe, prop_phase, amplitudes, offsets, counts, step_size):
    padded = jnp.pad(object_tiles, ((0, 0), (0, 0), (H, H), (H, H)))
    forward = dft_tables(P_SIZE, False)
    backward = dft_tables(P_SIZE, True)
    kernel_re = jnp.cos(prop_phase)
    kernel_im = jnp.sin(prop_phase)
    zero = jnp.int32(0)
    total = TROWS * TCOLS * MAXP

    def visit(grad, index):
        tile_row = (index // (TCOLS * MAXP)).astype(jnp.int32)
        tile_col = (index // MAXP % TCOLS).astype(jnp.int32)
        slot = (index % MAXP).astype(jnp.int32)
        start_row = (tile_row * TILE + offsets[tile_row, tile_col, slot, 0]).astype(jnp.int32)
        start_col = (tile_col * TILE + offsets[tile_row, tile_col, slot, 1]).astype(jnp.int32)
        corner = (zero, zero, start_row, start_col)

        def compute(unused):
            window = lax.dynamic_slice(padded, corner, (2, 2, P_SIZE, P_SIZE))
            return probe_gradient(window, probe, kernel_re, kernel_im, amplitudes[tile_row, tile_col, slot], forward, backward)

        def nothing(unused):
            return jnp.zeros((2, 2, P_SIZE, P_SIZE), jnp.float32)
        contribution = lax.cond(slot < counts[tile_row, tile_col], compute, nothing, 0)
        current = lax.dynamic_slice(grad, corner, (2, 2, P_SIZE, P_SIZE))
        return (lax.dynamic_update_slice(grad, current + contribution, corner), None)
    grad, unused = lax.scan(visit, jnp.zeros(padded.shape, jnp.float32), jnp.arange(total, dtype=jnp.int32))
    grad = grad[:, :, H:H + NR, H:H + NC]
    return object_tiles - step_size[:, None, None, None] * grad
```

```python
import functools
import math

import jax
import jax.numpy as jnp
import numpy as np
from jax import lax
from jax.experimental import pallas as pl
from jax.experimental.pallas import tpu as pltpu
from jax.sharding import PartitionSpec as P

H = 128
LANES = 128
SUBLANES = 8
ROWS = 256
F32 = jnp.float32
BF16 = jnp.bfloat16


def shifted(block, axis, step):
    count = lax.axis_size(axis)
    route = [(i, i + step) for i in range(count) if 0 <= i + step < count]
    return lax.ppermute(block, axis, route)


def dft_table(length):
    index = np.arange(length, dtype=np.int64)
    angles = ((index[:, None] * index[None, :]) % length).astype(np.float32) * np.float32(
        2.0 * math.pi / length
    )
    scaling = np.float32(1.0 / math.sqrt(length))
    return (
        jnp.asarray((np.cos(angles) * scaling).astype(BF16)),
        jnp.asarray((-np.sin(angles) * scaling).astype(BF16)),
    )


def params(flops=0, moved=0, mib=48):
    return dict(
        compiler_params=pltpu.CompilerParams(vmem_limit_bytes=mib << 20),
        cost_estimate=pl.CostEstimate(flops=flops, bytes_accessed=moved, transcendentals=0),
    )


SMEM = pl.BlockSpec(memory_space=pltpu.SMEM)
VMEM = pl.BlockSpec(memory_space=pltpu.VMEM)


def take_columns(wide, start, width):
    base = pl.multiple_of(start // LANES * LANES, LANES)
    piece = wide[:, pl.ds(base, width + LANES)]
    return pltpu.roll(piece, (width + LANES) - start % LANES, axis=1)[:, :width]


def edges_kernel(cols_ref, top, bottom, lt, lb, rt, rb, up, down, wide):
    inner = top.shape[-1]
    width = up.shape[-1]
    for left, tile, right, out, which in ((lt, top, rt, up, 1), (lb, bottom, rb, down, 2)):
        wide[:, :H] = left[0]
        wide[:, H : H + inner] = tile[0, 0]
        wide[:, H + inner : 2 * H + inner] = right[0]
        wide[:, 2 * H + inner :] = jnp.zeros((wide.shape[0], LANES), F32)
        out[0] = take_columns(wide, cols_ref[which], width)


def edges(cols, tile, left, right, s, width):
    rows, inner = tile.shape[2:]
    last = rows // H - 1
    side = lambda r: pl.BlockSpec((1, H, H), lambda c: (c, r, 0))
    return pl.pallas_call(
        edges_kernel,
        grid=(2,),
        in_specs=[
            SMEM,
            pl.BlockSpec((1, 1, H, inner), lambda c: (s, c, 0, 0)),
            pl.BlockSpec((1, 1, H, inner), lambda c: (s, c, last, 0)),
            side(0),
            side(last),
            side(0),
            side(last),
        ],
        out_specs=[pl.BlockSpec((1, H, width), lambda c: (c, 0, 0))] * 2,
        out_shape=[jax.ShapeDtypeStruct((2, H, width), F32)] * 2,
        scratch_shapes=[pltpu.VMEM((H, inner + 2 * H + LANES), F32)],
        name=f"edges{s}",
        **params(0, 3 << 20),
    )(cols, tile, tile, left, left, right, right)


def middle_kernel(cols_ref, tile, left, right, out, wide):
    inner = tile.shape[-1]
    wide[:, :H] = left[0]
    wide[:, H : H + inner] = tile[0, 0]
    wide[:, H + inner : 2 * H + inner] = right[0]
    wide[:, 2 * H + inner :] = jnp.zeros((wide.shape[0], LANES), F32)
    out[0] = take_columns(wide, cols_ref[0], out.shape[-1])


def middle(cols, tile, left, right, s, width):
    rows, inner = tile.shape[2:]
    return pl.pallas_call(
        middle_kernel,
        grid=(2, rows // H),
        in_specs=[
            SMEM,
            pl.BlockSpec((1, 1, H, inner), lambda c, r: (s, c, r, 0)),
            pl.BlockSpec((1, H, H), lambda c, r: (c, r, 0)),
            pl.BlockSpec((1, H, H), lambda c, r: (c, r, 0)),
        ],
        out_specs=pl.BlockSpec((1, H, width), lambda c, r: (c, r, 0)),
        out_shape=jax.ShapeDtypeStruct((2, rows, width), F32),
        scratch_shapes=[pltpu.VMEM((H, inner + 2 * H + LANES), F32)],
        name=f"middle{s}",
        **params(0, 9 << 20),
    )(cols, tile, left, right)


def make_tables(cos_ref, sin_ref, fwd, bwd):
    n = cos_ref.shape[0]
    c, s = cos_ref[...], sin_ref[...]
    for table, sine in ((fwd, s), (bwd, -s)):
        table[:n, :n] = c
        table[n:, n:] = c
        table[n:, :n] = sine
        table[:n, n:] = -sine


def transform(src, left, right, mid, epilogue):
    n = mid.shape[0]

    @pl.loop(0, n // ROWS)
    def _(i):
        at = pl.ds(pl.multiple_of(i * ROWS, ROWS), ROWS)
        low = pl.ds(pl.multiple_of(n + i * ROWS, ROWS), ROWS)
        mid[at, :n] = jnp.dot(left[at, :], src[...], preferred_element_type=F32).astype(BF16)
        mid[at, n:] = jnp.dot(left[low, :], src[...], preferred_element_type=F32).astype(BF16)

    @pl.loop(0, n // ROWS)
    def _(i):
        at = pl.ds(pl.multiple_of(i * ROWS, ROWS), ROWS)
        low = pl.ds(pl.multiple_of(n + i * ROWS, ROWS), ROWS)
        out = jnp.dot(mid[at, :], right[...], preferred_element_type=F32)
        epilogue(i, at, low, out[:, :n], out[:, n:])


def take_rows(field, part, start, offset, height):
    base = pl.multiple_of(start // SUBLANES * SUBLANES + offset, SUBLANES)
    piece = field[part, pl.ds(base, height + SUBLANES), :]
    return pltpu.roll(piece, (height + SUBLANES) - start % SUBLANES, axis=0)[:height]


def add_rows(field, part, start, offset, block):
    height = block.shape[0]
    base = pl.multiple_of(start // SUBLANES * SUBLANES + offset, SUBLANES)
    block = jnp.concatenate([block, jnp.zeros((SUBLANES, block.shape[1]), F32)], axis=0)
    field[part, pl.ds(base, height + SUBLANES), :] += pltpu.roll(block, start % SUBLANES, axis=0)


def load_window(top, body, bottom, window):
    rows = body.shape[1]
    window[:, :H] = top[...]
    window[:, H : H + rows] = body[...]
    window[:, H + rows : 2 * H + rows] = bottom[...]


def first_kernel(rows_ref, top, body, bottom, probe, k, cos, sin, psi, window, fwd, bwd, src, mid):
    n = cos.shape[0]
    make_tables(cos, sin, fwd, bwd)
    load_window(top, body, bottom, window)
    start = rows_ref[0]

    @pl.loop(0, n // H)
    def _(i):
        at = pl.ds(pl.multiple_of(i * H, H), H)
        low = pl.ds(pl.multiple_of(n + i * H, H), H)
        a_re = take_rows(window, 0, start, i * H, H)
        a_im = take_rows(window, 1, start, i * H, H)
        q_re, q_im = probe[0, at, :], probe[1, at, :]
        src[at, :] = (q_re * a_re - q_im * a_im).astype(BF16)
        src[low, :] = (q_re * a_im + q_im * a_re).astype(BF16)

    def propagate(i, at, low, re, im):
        k_re, k_im = k[0, at, :], k[1, at, :]
        src[at, :] = (re * k_re - im * k_im).astype(BF16)
        src[low, :] = (re * k_im + im * k_re).astype(BF16)

    def keep(i, at, low, re, im):
        psi[0, at, :] = re
        psi[1, at, :] = im

    transform(src, fwd, bwd, mid, propagate)
    transform(src, bwd, fwd, mid, keep)


def second_kernel(
    rows_ref, count_ref, top, body, bottom, psi, amp, cos, sin, grad, back, window, fwd, bwd, src, mid
):
    n = cos.shape[0]
    make_tables(cos, sin, fwd, bwd)
    load_window(top, body, bottom, window)
    start = rows_ref[0]
    weight = jnp.where(count_ref[0] > 0, 1.0, 0.0).astype(F32)
    grad[...] = jnp.zeros_like(grad)

    @pl.loop(0, n // H)
    def _(i):
        at = pl.ds(pl.multiple_of(i * H, H), H)
        low = pl.ds(pl.multiple_of(n + i * H, H), H)
        b_re = take_rows(window, 0, start, i * H, H)
        b_im = take_rows(window, 1, start, i * H, H)
        p_re, p_im = psi[0, at, :], psi[1, at, :]
        src[at, :] = (p_re * b_re - p_im * b_im).astype(BF16)
        src[low, :] = (p_re * b_im + p_im * b_re).astype(BF16)

    def detect(i, at, low, re, im):
        factor = 1.0 - amp[at, :].astype(F32) / jnp.sqrt(re * re + im * im + 1.0)
        src[at, :] = (re * factor).astype(BF16)
        src[low, :] = (im * factor).astype(BF16)

    def spread(i, at, low, re, im):
        p_re, p_im = psi[0, at, :], psi[1, at, :]
        b_re = take_rows(window, 0, start, i * ROWS, ROWS)
        b_im = take_rows(window, 1, start, i * ROWS, ROWS)
        add_rows(grad, 0, start, i * ROWS, weight * (p_re * re + p_im * im))
        add_rows(grad, 1, start, i * ROWS, weight * (p_re * im - p_im * re))
        back[at, :] = (b_re * re + b_im * im).astype(BF16)
        back[low, :] = (b_re * im - b_im * re).astype(BF16)

    transform(src, fwd, bwd, mid, detect)
    transform(src, bwd, fwd, mid, spread)


def third_kernel(rows_ref, count_ref, back, probe, k, cos, sin, grad, fwd, bwd, src, mid):
    make_tables(cos, sin, fwd, bwd)
    start = rows_ref[0]
    weight = jnp.where(count_ref[0] > 0, 1.0, 0.0).astype(F32)
    grad[...] = jnp.zeros_like(grad)

    def propagate(i, at, low, re, im):
        k_re, k_im = k[0, at, :], k[1, at, :]
        src[at, :] = (re * k_re + im * k_im).astype(BF16)
        src[low, :] = (im * k_re - re * k_im).astype(BF16)

    def finish(i, at, low, re, im):
        q_re, q_im = probe[0, at, :], probe[1, at, :]
        add_rows(grad, 0, start, i * ROWS, weight * (q_re * re + q_im * im))
        add_rows(grad, 1, start, i * ROWS, weight * (q_re * im - q_im * re))

    transform(back, fwd, bwd, mid, propagate)
    transform(src, bwd, fwd, mid, finish)


def work(n):
    return [
        pltpu.VMEM((2 * n, 2 * n), BF16),
        pltpu.VMEM((2 * n, 2 * n), BF16),
        pltpu.VMEM((2 * n, n), BF16),
        pltpu.VMEM((n, 2 * n), BF16),
    ]


def place_kernel(s, cols_ref, step_ref, grad, above, below, tile, *rest):
    out, to_left, to_right, wide = rest[-4:]
    rows, inner = tile.shape[2:]
    width = grad.shape[-1]
    wide[...] = jnp.zeros_like(wide)

    def add(row, block, start):
        base = pl.multiple_of(start // LANES * LANES, LANES)
        block = jnp.concatenate([block, jnp.zeros((H, LANES), F32)], axis=1)
        wide[pl.ds(row, H), pl.ds(base, width + LANES)] += pltpu.roll(block, start % LANES, axis=1)

    @pl.loop(0, rows // H)
    def _(i):
        add(pl.multiple_of(i * H, H), grad[0, pl.ds(pl.multiple_of(H + i * H, H), H), :], cols_ref[0])

    add(0, above[0], cols_ref[1])
    add(rows - H, below[0], cols_ref[2])
    out[0, 0] = tile[0, 0] - step_ref[s] * wide[:, H : H + inner]
    to_left[0] = wide[:, :H]
    to_right[0] = wide[:, H + inner : 2 * H + inner]


def place(cols, step, grad, above, below, tile, s, so_far):
    rows, inner = tile.shape[2:]
    width = grad.shape[-1]
    plane = pl.BlockSpec((1, 1, rows, inner), lambda c: (s, c, 0, 0))
    edge = pl.BlockSpec((1, H, width), lambda c: (c, 0, 0))
    side = pl.BlockSpec((1, rows, H), lambda c: (c, 0, 0))
    more = [] if so_far is None else [so_far]
    return pl.pallas_call(
        functools.partial(place_kernel, s),
        grid=(2,),
        in_specs=[SMEM, SMEM, pl.BlockSpec((1,) + grad.shape[1:], lambda c: (c, 0, 0)), edge, edge, plane]
        + [pl.BlockSpec(memory_space=pl.ANY)] * len(more),
        out_specs=[plane, side, side],
        out_shape=[
            jax.ShapeDtypeStruct(tile.shape, F32),
            jax.ShapeDtypeStruct((2, rows, H), F32),
            jax.ShapeDtypeStruct((2, rows, H), F32),
        ],
        scratch_shapes=[pltpu.VMEM((rows, inner + 2 * H + LANES), F32)],
        input_output_aliases={6: 0} if more else {},
        name=f"place{s}",
        **params(0, 14 << 20),
    )(cols, step, grad, above, below, tile, *more)


def border_kernel(s, step_ref, left, right, old, out):
    @pl.when(pl.program_id(1) == 0)
    def _():
        out[0, 0] = old[0, 0] - step_ref[s] * left[0]

    @pl.when(pl.program_id(1) == 1)
    def _():
        out[0, 0] = old[0, 0] - step_ref[s] * right[0]


def border(step, left, right, out, s):
    rows, inner = out.shape[2:]
    far = inner // H - 1
    strip = pl.BlockSpec((1, 1, rows, H), lambda c, e: (s, c, 0, e * far))
    side = pl.BlockSpec((1, rows, H), lambda c, e: (c, 0, 0))
    return pl.pallas_call(
        functools.partial(border_kernel, s),
        grid=(2, 2),
        in_specs=[SMEM, side, side, strip],
        out_specs=strip,
        out_shape=jax.ShapeDtypeStruct(out.shape, F32),
        input_output_aliases={3: 0},
        name=f"border{s}",
        **params(0, 5 << 20),
    )(step, left, right, out)


def per_device(object_tiles, probe, prop_phase, amplitudes, offsets, counts, step_size):
    n = probe.shape[1]
    rows, inner = object_tiles.shape[2:]
    cos, sin = dft_table(n)
    kernel = jnp.stack([jnp.cos(prop_phase), jnp.sin(prop_phase)])
    mine = offsets[0, 0, 0]
    above = shifted(mine, "rows", 1)
    below = shifted(mine, "rows", -1)
    cols = jnp.stack([mine[1], above[1], below[1]])
    row = mine[:1]
    count = counts[0]

    lefts, rights, tops, bottoms, bodies = [], [], [], [], []
    for s in range(2):
        lefts.append(shifted(object_tiles[s, :, :, inner - H :], "cols", 1))
        rights.append(shifted(object_tiles[s, :, :, :H], "cols", -1))
    for s in range(2):
        up, down = edges(cols, object_tiles, lefts[s], rights[s], s, n)
        tops.append(shifted(down, "rows", 1))
        bottoms.append(shifted(up, "rows", -1))
    for s in range(2):
        bodies.append(middle(cols, object_tiles, lefts[s], rights[s], s, n))

    per_transform = 2 * 2 * (2 * n) * (2 * n) * n
    ext = jax.ShapeDtypeStruct((2, rows + 2 * H + SUBLANES, n), F32)
    field = jax.ShapeDtypeStruct((2, n, n), F32)
    window = pltpu.VMEM(ext.shape, F32)
    psi = pl.pallas_call(
        first_kernel,
        in_specs=[SMEM] + [VMEM] * 7,
        out_specs=VMEM,
        out_shape=field,
        scratch_shapes=[window] + work(n),
        name="first",
        **params(2 * per_transform, 12 << 20),
    )(row, tops[0], bodies[0], bottoms[0], probe, kernel, cos, sin)
    grad2, back = pl.pallas_call(
        second_kernel,
        in_specs=[SMEM] * 2 + [VMEM] * 7,
        out_specs=[VMEM, VMEM],
        out_shape=[ext, jax.ShapeDtypeStruct((2 * n, n), BF16)],
        scratch_shapes=[window] + work(n),
        name="second",
        **params(2 * per_transform, 14 << 20),
    )(row, count, tops[1], bodies[1], bottoms[1], psi, amplitudes[0, 0, 0], cos, sin)
    grad1 = pl.pallas_call(
        third_kernel,
        in_specs=[SMEM] * 2 + [VMEM] * 5,
        out_specs=VMEM,
        out_shape=ext,
        scratch_shapes=work(n),
        name="third",
        **params(2 * per_transform, 12 << 20),
    )(row, count, back, probe, kernel, cos, sin)

    out = None
    sides = []
    for s, grad in ((1, grad2), (0, grad1)):
        from_above = shifted(grad[:, rows + H : rows + 2 * H], "rows", 1)
        from_below = shifted(grad[:, :H], "rows", -1)
        out, to_left, to_right = place(
            cols, step_size, grad, from_above, from_below, object_tiles, s, out
        )
        sides.append((s, shifted(to_right, "cols", 1), shifted(to_left, "cols", -1)))
    for s, left, right in sides:
        out = border(step_size, left, right, out, s)
    return out


def solution(mesh):
    return jax.shard_map(
        per_device,
        mesh=mesh,
        in_specs=(
            P(None, None, "rows", "cols"),
            P(),
            P(),
            P("rows", "cols", None, None, None),
            P("rows", "cols", None, None),
            P("rows", "cols"),
            P(),
        ),
        out_specs=P(None, None, "rows", "cols"),
        check_vma=False,
    )
```

```python
import functools
import math

import jax
import jax.numpy as jnp
import numpy as np
from jax import lax
from jax.experimental import pallas as pl
from jax.experimental.pallas import tpu as pltpu
from jax.sharding import PartitionSpec as P

H = 128
LANES = 128
SUBLANES = 8
ROWS = 256
F32 = jnp.float32
BF16 = jnp.bfloat16


def shifted(block, axis, step):
    count = lax.axis_size(axis)
    route = [(i, i + step) for i in range(count) if 0 <= i + step < count]
    return lax.ppermute(block, axis, route)


def dft_table(length):
    index = np.arange(length, dtype=np.int64)
    angles = ((index[:, None] * index[None, :]) % length).astype(np.float32) * np.float32(
        2.0 * math.pi / length
    )
    scaling = np.float32(1.0 / math.sqrt(length))
    return (
        jnp.asarray((np.cos(angles) * scaling).astype(BF16)),
        jnp.asarray((-np.sin(angles) * scaling).astype(BF16)),
    )


def params(flops=0, moved=0, mib=48):
    return dict(
        compiler_params=pltpu.CompilerParams(vmem_limit_bytes=mib << 20),
        cost_estimate=pl.CostEstimate(flops=flops, bytes_accessed=moved, transcendentals=0),
    )


SMEM = pl.BlockSpec(memory_space=pltpu.SMEM)
VMEM = pl.BlockSpec(memory_space=pltpu.VMEM)


def take_columns(wide, start, width):
    base = pl.multiple_of(start // LANES * LANES, LANES)
    piece = wide[:, pl.ds(base, width + LANES)]
    return pltpu.roll(piece, (width + LANES) - start % LANES, axis=1)[:, :width]


def edges_kernel(cols_ref, top, bottom, lt, lb, rt, rb, up, down, wide):
    inner = top.shape[-1]
    width = up.shape[-1]
    for left, tile, right, out, which in ((lt, top, rt, up, 1), (lb, bottom, rb, down, 2)):
        wide[:, :H] = left[0, 0]
        wide[:, H : H + inner] = tile[0, 0]
        wide[:, H + inner : 2 * H + inner] = right[0, 0]
        wide[:, 2 * H + inner :] = jnp.zeros((wide.shape[0], LANES), F32)
        out[0, 0] = take_columns(wide, cols_ref[which], width)


def edges(cols, tile, left, right, width):
    rows, inner = tile.shape[2:]
    last = rows // H - 1
    side = lambda r: pl.BlockSpec((1, 1, H, H), lambda s, c: (s, c, r, 0))
    return pl.pallas_call(
        edges_kernel,
        grid=(2, 2),
        in_specs=[
            SMEM,
            pl.BlockSpec((1, 1, H, inner), lambda s, c: (s, c, 0, 0)),
            pl.BlockSpec((1, 1, H, inner), lambda s, c: (s, c, last, 0)),
            side(0),
            side(last),
            side(0),
            side(last),
        ],
        out_specs=[pl.BlockSpec((1, 1, H, width), lambda s, c: (s, c, 0, 0))] * 2,
        out_shape=[jax.ShapeDtypeStruct((2, 2, H, width), F32)] * 2,
        scratch_shapes=[pltpu.VMEM((H, inner + 2 * H + LANES), F32)],
        name="edges",
        **params(0, 5 << 20),
    )(cols, tile, tile, left, left, right, right)


def middle_kernel(cols_ref, tile, left, right, out, wide):
    inner = tile.shape[-1]
    wide[:, :H] = left[0, 0]
    wide[:, H : H + inner] = tile[0, 0]
    wide[:, H + inner : 2 * H + inner] = right[0, 0]
    wide[:, 2 * H + inner :] = jnp.zeros((wide.shape[0], LANES), F32)
    out[0] = take_columns(wide, cols_ref[0], out.shape[-1])


def middle(cols, tile, left, right, s, width):
    rows, inner = tile.shape[2:]
    return pl.pallas_call(
        middle_kernel,
        grid=(2,),
        in_specs=[
            SMEM,
            pl.BlockSpec((1, 1, rows, inner), lambda c: (s, c, 0, 0)),
            pl.BlockSpec((1, 1, rows, H), lambda c: (s, c, 0, 0)),
            pl.BlockSpec((1, 1, rows, H), lambda c: (s, c, 0, 0)),
        ],
        out_specs=pl.BlockSpec((1, rows, width), lambda c: (c, 0, 0)),
        out_shape=jax.ShapeDtypeStruct((2, rows, width), F32),
        scratch_shapes=[pltpu.VMEM((rows, inner + 2 * H + LANES), F32)],
        name=f"middle{s}",
        **params(0, 9 << 20),
    )(cols, tile, left, right)


def make_tables(cos_ref, sin_ref, fwd, bwd):
    n = cos_ref.shape[0]
    c, s = cos_ref[...], sin_ref[...]
    for table, sine in ((fwd, s), (bwd, -s)):
        table[:n, :n] = c
        table[n:, n:] = c
        table[n:, :n] = sine
        table[:n, n:] = -sine


def transform(src, left, right, mid, epilogue):
    n = mid.shape[0]

    @pl.loop(0, n // ROWS)
    def _(i):
        at = pl.ds(pl.multiple_of(i * ROWS, ROWS), ROWS)
        low = pl.ds(pl.multiple_of(n + i * ROWS, ROWS), ROWS)
        mid[at, :n] = jnp.dot(left[at, :], src[...], preferred_element_type=F32).astype(BF16)
        mid[at, n:] = jnp.dot(left[low, :], src[...], preferred_element_type=F32).astype(BF16)

    @pl.loop(0, n // ROWS)
    def _(i):
        at = pl.ds(pl.multiple_of(i * ROWS, ROWS), ROWS)
        low = pl.ds(pl.multiple_of(n + i * ROWS, ROWS), ROWS)
        out = jnp.dot(mid[at, :], right[...], preferred_element_type=F32)
        epilogue(i, at, low, out[:, :n], out[:, n:])


def take_rows(field, part, start, offset, height):
    base = pl.multiple_of(start // SUBLANES * SUBLANES + offset, SUBLANES)
    piece = field[part, pl.ds(base, height + SUBLANES), :]
    return pltpu.roll(piece, (height + SUBLANES) - start % SUBLANES, axis=0)[:height]


def add_rows(field, part, start, offset, block):
    height = block.shape[0]
    base = pl.multiple_of(start // SUBLANES * SUBLANES + offset, SUBLANES)
    block = jnp.concatenate([block, jnp.zeros((SUBLANES, block.shape[1]), F32)], axis=0)
    field[part, pl.ds(base, height + SUBLANES), :] += pltpu.roll(block, start % SUBLANES, axis=0)


def load_window(top, body, bottom, window):
    rows = body.shape[1]
    window[:, :H] = top[...]
    window[:, H : H + rows] = body[...]
    window[:, H + rows : 2 * H + rows] = bottom[...]


def first_kernel(rows_ref, top, body, bottom, probe, k, cos, sin, psi, window, fwd, bwd, src, mid):
    n = cos.shape[0]
    make_tables(cos, sin, fwd, bwd)
    load_window(top, body, bottom, window)
    start = rows_ref[0]

    @pl.loop(0, n // H)
    def _(i):
        at = pl.ds(pl.multiple_of(i * H, H), H)
        low = pl.ds(pl.multiple_of(n + i * H, H), H)
        a_re = take_rows(window, 0, start, i * H, H)
        a_im = take_rows(window, 1, start, i * H, H)
        q_re, q_im = probe[0, at, :], probe[1, at, :]
        src[at, :] = (q_re * a_re - q_im * a_im).astype(BF16)
        src[low, :] = (q_re * a_im + q_im * a_re).astype(BF16)

    def propagate(i, at, low, re, im):
        k_re, k_im = k[0, at, :], k[1, at, :]
        src[at, :] = (re * k_re - im * k_im).astype(BF16)
        src[low, :] = (re * k_im + im * k_re).astype(BF16)

    def keep(i, at, low, re, im):
        psi[0, at, :] = re
        psi[1, at, :] = im

    transform(src, fwd, bwd, mid, propagate)
    transform(src, bwd, fwd, mid, keep)


def second_kernel(
    rows_ref, count_ref, top, body, bottom, psi, amp, cos, sin, grad, back, window, fwd, bwd, src, mid
):
    n = cos.shape[0]
    make_tables(cos, sin, fwd, bwd)
    load_window(top, body, bottom, window)
    start = rows_ref[0]
    weight = jnp.where(count_ref[0] > 0, 1.0, 0.0).astype(F32)
    grad[...] = jnp.zeros_like(grad)

    @pl.loop(0, n // H)
    def _(i):
        at = pl.ds(pl.multiple_of(i * H, H), H)
        low = pl.ds(pl.multiple_of(n + i * H, H), H)
        b_re = take_rows(window, 0, start, i * H, H)
        b_im = take_rows(window, 1, start, i * H, H)
        p_re, p_im = psi[0, at, :], psi[1, at, :]
        src[at, :] = (p_re * b_re - p_im * b_im).astype(BF16)
        src[low, :] = (p_re * b_im + p_im * b_re).astype(BF16)

    def detect(i, at, low, re, im):
        factor = 1.0 - amp[at, :].astype(F32) / jnp.sqrt(re * re + im * im + 1.0)
        src[at, :] = (re * factor).astype(BF16)
        src[low, :] = (im * factor).astype(BF16)

    def spread(i, at, low, re, im):
        p_re, p_im = psi[0, at, :], psi[1, at, :]
        b_re = take_rows(window, 0, start, i * ROWS, ROWS)
        b_im = take_rows(window, 1, start, i * ROWS, ROWS)
        add_rows(grad, 0, start, i * ROWS, weight * (p_re * re + p_im * im))
        add_rows(grad, 1, start, i * ROWS, weight * (p_re * im - p_im * re))
        back[at, :] = (b_re * re + b_im * im).astype(BF16)
        back[low, :] = (b_re * im - b_im * re).astype(BF16)

    transform(src, fwd, bwd, mid, detect)
    transform(src, bwd, fwd, mid, spread)


def third_kernel(rows_ref, count_ref, back, probe, k, cos, sin, grad, fwd, bwd, src, mid):
    make_tables(cos, sin, fwd, bwd)
    start = rows_ref[0]
    weight = jnp.where(count_ref[0] > 0, 1.0, 0.0).astype(F32)
    grad[...] = jnp.zeros_like(grad)

    def propagate(i, at, low, re, im):
        k_re, k_im = k[0, at, :], k[1, at, :]
        src[at, :] = (re * k_re + im * k_im).astype(BF16)
        src[low, :] = (im * k_re - re * k_im).astype(BF16)

    def finish(i, at, low, re, im):
        q_re, q_im = probe[0, at, :], probe[1, at, :]
        add_rows(grad, 0, start, i * ROWS, weight * (q_re * re + q_im * im))
        add_rows(grad, 1, start, i * ROWS, weight * (q_re * im - q_im * re))

    transform(back, fwd, bwd, mid, propagate)
    transform(src, bwd, fwd, mid, finish)


def work(n):
    return [
        pltpu.VMEM((2 * n, 2 * n), BF16),
        pltpu.VMEM((2 * n, 2 * n), BF16),
        pltpu.VMEM((2 * n, n), BF16),
        pltpu.VMEM((n, 2 * n), BF16),
    ]


def gather(cols_ref, grad, above, below, wide):
    rows = wide.shape[0]
    width = grad.shape[-1]
    wide[...] = jnp.zeros_like(wide)

    def add(row, block, start):
        base = pl.multiple_of(start // LANES * LANES, LANES)
        block = jnp.concatenate([block, jnp.zeros((H, LANES), F32)], axis=1)
        wide[pl.ds(row, H), pl.ds(base, width + LANES)] += pltpu.roll(block, start % LANES, axis=1)

    @pl.loop(0, rows // H)
    def _(i):
        add(pl.multiple_of(i * H, H), grad[0, pl.ds(pl.multiple_of(H + i * H, H), H), :], cols_ref[0])

    add(0, above[0], cols_ref[1])
    add(rows - H, below[0], cols_ref[2])


def spill_kernel(cols_ref, grad, above, below, to_left, to_right, wide):
    inner = wide.shape[1] - 2 * H - LANES
    gather(cols_ref, grad, above, below, wide)
    to_left[0] = wide[:, :H]
    to_right[0] = wide[:, H + inner : 2 * H + inner]


def place_kernel(s, cols_ref, step_ref, grad, above, below, left, right, tile, *rest):
    out, wide = rest[-2:]
    inner = tile.shape[-1]
    gather(cols_ref, grad, above, below, wide)
    wide[:, H : 2 * H] += left[0]
    wide[:, inner : H + inner] += right[0]
    out[0, 0] = tile[0, 0] - step_ref[s] * wide[:, H : H + inner]


def gradient_specs(grad, rows):
    edge = pl.BlockSpec((1, H, grad.shape[-1]), lambda c: (c, 0, 0))
    side = pl.BlockSpec((1, rows, H), lambda c: (c, 0, 0))
    return [pl.BlockSpec((1,) + grad.shape[1:], lambda c: (c, 0, 0)), edge, edge], [side, side]


def spill(cols, grad, above, below, tile, s):
    rows, inner = tile.shape[2:]
    sources, sides = gradient_specs(grad, rows)
    return pl.pallas_call(
        spill_kernel,
        grid=(2,),
        in_specs=[SMEM] + sources,
        out_specs=sides,
        out_shape=[jax.ShapeDtypeStruct((2, rows, H), F32)] * 2,
        scratch_shapes=[pltpu.VMEM((rows, inner + 2 * H + LANES), F32)],
        name=f"spill{s}",
        **params(0, 7 << 20),
    )(cols, grad, above, below)


def place(cols, step, grad, above, below, left, right, tile, s, so_far):
    rows, inner = tile.shape[2:]
    sources, sides = gradient_specs(grad, rows)
    plane = pl.BlockSpec((1, 1, rows, inner), lambda c: (s, c, 0, 0))
    more = [] if so_far is None else [so_far]
    return pl.pallas_call(
        functools.partial(place_kernel, s),
        grid=(2,),
        in_specs=[SMEM, SMEM] + sources + sides + [plane] + [pl.BlockSpec(memory_space=pl.ANY)] * len(more),
        out_specs=plane,
        out_shape=jax.ShapeDtypeStruct(tile.shape, F32),
        scratch_shapes=[pltpu.VMEM((rows, inner + 2 * H + LANES), F32)],
        input_output_aliases={8: 0} if more else {},
        name=f"place{s}",
        **params(0, 14 << 20),
    )(cols, step, grad, above, below, left, right, tile, *more)


def per_device(object_tiles, probe, prop_phase, amplitudes, offsets, counts, step_size):
    n = probe.shape[1]
    rows, inner = object_tiles.shape[2:]
    cos, sin = dft_table(n)
    kernel = jnp.stack([jnp.cos(prop_phase), jnp.sin(prop_phase)])
    mine = offsets[0, 0, 0]
    above = shifted(mine, "rows", 1)
    below = shifted(mine, "rows", -1)
    cols = jnp.stack([mine[1], above[1], below[1]])
    row = mine[:1]
    count = counts[0]

    left = shifted(object_tiles[:, :, :, inner - H :], "cols", 1)
    right = shifted(object_tiles[:, :, :, :H], "cols", -1)
    up, down = edges(cols, object_tiles, left, right, n)
    tops = [shifted(down[s], "rows", 1) for s in range(2)]
    bottoms = [shifted(up[s], "rows", -1) for s in range(2)]
    bodies = [middle(cols, object_tiles, left, right, s, n) for s in range(2)]

    per_transform = 2 * 2 * (2 * n) * (2 * n) * n
    ext = jax.ShapeDtypeStruct((2, rows + 2 * H + SUBLANES, n), F32)
    field = jax.ShapeDtypeStruct((2, n, n), F32)
    window = pltpu.VMEM(ext.shape, F32)
    psi = pl.pallas_call(
        first_kernel,
        in_specs=[SMEM] + [VMEM] * 7,
        out_specs=VMEM,
        out_shape=field,
        scratch_shapes=[window] + work(n),
        name="first",
        **params(2 * per_transform, 12 << 20),
    )(row, tops[0], bodies[0], bottoms[0], probe, kernel, cos, sin)
    grad2, back = pl.pallas_call(
        second_kernel,
        in_specs=[SMEM] * 2 + [VMEM] * 7,
        out_specs=[VMEM, VMEM],
        out_shape=[ext, jax.ShapeDtypeStruct((2 * n, n), BF16)],
        scratch_shapes=[window] + work(n),
        name="second",
        **params(2 * per_transform, 14 << 20),
    )(row, count, tops[1], bodies[1], bottoms[1], psi, amplitudes[0, 0, 0], cos, sin)
    grad1 = pl.pallas_call(
        third_kernel,
        in_specs=[SMEM] * 2 + [VMEM] * 5,
        out_specs=VMEM,
        out_shape=ext,
        scratch_shapes=work(n),
        name="third",
        **params(2 * per_transform, 12 << 20),
    )(row, count, back, probe, kernel, cos, sin)

    parts = []
    for s, grad in ((1, grad2), (0, grad1)):
        from_above = shifted(grad[:, rows + H : rows + 2 * H], "rows", 1)
        from_below = shifted(grad[:, :H], "rows", -1)
        to_left, to_right = spill(cols, grad, from_above, from_below, object_tiles, s)
        from_left, from_right = shifted(to_right, "cols", 1), shifted(to_left, "cols", -1)
        parts.append((s, (grad, from_above, from_below, from_left, from_right)))
    out = None
    for s, pieces in parts:
        out = place(cols, step_size, *pieces, object_tiles, s, out)
    return out


def solution(mesh):
    return jax.shard_map(
        per_device,
        mesh=mesh,
        in_specs=(
            P(None, None, "rows", "cols"),
            P(),
            P(),
            P("rows", "cols", None, None, None),
            P("rows", "cols", None, None),
            P("rows", "cols"),
            P(),
        ),
        out_specs=P(None, None, "rows", "cols"),
        check_vma=False,
    )
```

```python
import functools
import math

import jax
import jax.numpy as jnp
import numpy as np
from jax import lax
from jax.experimental import pallas as pl
from jax.experimental.pallas import tpu as pltpu
from jax.sharding import PartitionSpec as P


H = 128
LANES = 128
SUBLANES = 8
ROWS = 512
F32 = jnp.float32
BF16 = jnp.bfloat16


def shifted(block, axis, step):
    count = lax.axis_size(axis)
    route = [(i, i + step) for i in range(count) if 0 <= i + step < count]
    return lax.ppermute(block, axis, route)


def dft_table(length):
    index = np.arange(length, dtype=np.int64)
    angles = ((index[:, None] * index[None, :]) % length).astype(np.float32) * np.float32(
        2.0 * math.pi / length
    )
    scaling = np.float32(1.0 / math.sqrt(length))
    return (
        jnp.asarray((np.cos(angles) * scaling).astype(BF16)),
        jnp.asarray((-np.sin(angles) * scaling).astype(BF16)),
    )


def params(flops=0, moved=0, mib=48):
    return dict(
        compiler_params=pltpu.CompilerParams(vmem_limit_bytes=mib << 20),
        cost_estimate=pl.CostEstimate(flops=flops, bytes_accessed=moved, transcendentals=0),
    )


SMEM = pl.BlockSpec(memory_space=pltpu.SMEM)
VMEM = pl.BlockSpec(memory_space=pltpu.VMEM)


def take_columns(wide, start, width):
    base = pl.multiple_of(start // LANES * LANES, LANES)
    piece = wide[:, pl.ds(base, width + LANES)]
    return pltpu.roll(piece, (width + LANES) - start % LANES, axis=1)[:, :width]


def edges_kernel(cols_ref, top, bottom, lt, lb, rt, rb, up, down, wide):
    inner = top.shape[-1]
    width = up.shape[-1]
    for left, tile, right, out, which in ((lt, top, rt, up, 1), (lb, bottom, rb, down, 2)):
        wide[:, :H] = left[0]
        wide[:, H : H + inner] = tile[0, 0]
        wide[:, H + inner : 2 * H + inner] = right[0]
        wide[:, 2 * H + inner :] = jnp.zeros((wide.shape[0], LANES), F32)
        out[0] = take_columns(wide, cols_ref[which], width)


def edges(cols, tile, left, right, s, width):
    rows, inner = tile.shape[2:]
    last = rows // H - 1
    side = lambda r: pl.BlockSpec((1, H, H), lambda c: (c, r, 0))
    return pl.pallas_call(
        edges_kernel,
        grid=(2,),
        in_specs=[
            SMEM,
            pl.BlockSpec((1, 1, H, inner), lambda c: (s, c, 0, 0)),
            pl.BlockSpec((1, 1, H, inner), lambda c: (s, c, last, 0)),
            side(0),
            side(last),
            side(0),
            side(last),
        ],
        out_specs=[pl.BlockSpec((1, H, width), lambda c: (c, 0, 0))] * 2,
        out_shape=[jax.ShapeDtypeStruct((2, H, width), F32)] * 2,
        scratch_shapes=[pltpu.VMEM((H, inner + 2 * H + LANES), F32)],
        **params(0, 3 << 20),
    )(cols, tile, tile, left, left, right, right)


def middle_kernel(cols_ref, tile, left, right, out, wide):
    inner = tile.shape[-1]
    wide[:, :H] = left[0]
    wide[:, H : H + inner] = tile[0, 0]
    wide[:, H + inner : 2 * H + inner] = right[0]
    wide[:, 2 * H + inner :] = jnp.zeros((wide.shape[0], LANES), F32)
    out[0] = take_columns(wide, cols_ref[0], out.shape[-1])


def middle(cols, tile, left, right, s, width):
    rows, inner = tile.shape[2:]
    return pl.pallas_call(
        middle_kernel,
        grid=(2,),
        in_specs=[
            SMEM,
            pl.BlockSpec((1, 1, rows, inner), lambda c: (s, c, 0, 0)),
            pl.BlockSpec((1, rows, H), lambda c: (c, 0, 0)),
            pl.BlockSpec((1, rows, H), lambda c: (c, 0, 0)),
        ],
        out_specs=pl.BlockSpec((1, rows, width), lambda c: (c, 0, 0)),
        out_shape=jax.ShapeDtypeStruct((2, rows, width), F32),
        scratch_shapes=[pltpu.VMEM((rows, inner + 2 * H + LANES), F32)],
        **params(0, 9 << 20),
    )(cols, tile, left, right)


def make_tables(cos_ref, sin_ref, fwd, bwd):
    n = cos_ref.shape[0]
    c, s = cos_ref[...], sin_ref[...]
    for table, sine in ((fwd, s), (bwd, -s)):
        table[:n, :n] = c
        table[n:, n:] = c
        table[n:, :n] = sine
        table[:n, n:] = -sine


def transform(src, left, right, mid, epilogue):
    n = mid.shape[0]

    @pl.loop(0, n // ROWS)
    def _(i):
        at = pl.ds(pl.multiple_of(i * ROWS, ROWS), ROWS)
        low = pl.ds(pl.multiple_of(n + i * ROWS, ROWS), ROWS)
        mid[at, :n] = jnp.dot(left[at, :], src[...], preferred_element_type=F32).astype(BF16)
        mid[at, n:] = jnp.dot(left[low, :], src[...], preferred_element_type=F32).astype(BF16)

    @pl.loop(0, n // ROWS)
    def _(i):
        at = pl.ds(pl.multiple_of(i * ROWS, ROWS), ROWS)
        low = pl.ds(pl.multiple_of(n + i * ROWS, ROWS), ROWS)
        out = jnp.dot(mid[at, :], right[...], preferred_element_type=F32)
        epilogue(i, at, low, out[:, :n], out[:, n:])


def take_rows(field, part, start, offset, height):
    base = pl.multiple_of(start // SUBLANES * SUBLANES + offset, SUBLANES)
    piece = field[part, pl.ds(base, height + SUBLANES), :]
    return pltpu.roll(piece, (height + SUBLANES) - start % SUBLANES, axis=0)[:height]


def add_rows(field, part, start, offset, block):
    height = block.shape[0]
    base = pl.multiple_of(start // SUBLANES * SUBLANES + offset, SUBLANES)
    block = jnp.concatenate([block, jnp.zeros((SUBLANES, block.shape[1]), F32)], axis=0)
    field[part, pl.ds(base, height + SUBLANES), :] += pltpu.roll(block, start % SUBLANES, axis=0)


def load_window(top, body, bottom, window):
    rows = body.shape[1]
    window[:, :H] = top[...]
    window[:, H : H + rows] = body[...]
    window[:, H + rows : 2 * H + rows] = bottom[...]


def first_kernel(rows_ref, top, body, bottom, probe, k, cos, sin, psi, window, fwd, bwd, src, mid):
    n = cos.shape[0]
    make_tables(cos, sin, fwd, bwd)
    load_window(top, body, bottom, window)
    start = rows_ref[0]

    @pl.loop(0, n // H)
    def _(i):
        at = pl.ds(pl.multiple_of(i * H, H), H)
        low = pl.ds(pl.multiple_of(n + i * H, H), H)
        a_re = take_rows(window, 0, start, i * H, H)
        a_im = take_rows(window, 1, start, i * H, H)
        q_re, q_im = probe[0, at, :], probe[1, at, :]
        src[at, :] = (q_re * a_re - q_im * a_im).astype(BF16)
        src[low, :] = (q_re * a_im + q_im * a_re).astype(BF16)

    def propagate(i, at, low, re, im):
        k_re, k_im = k[0, at, :], k[1, at, :]
        src[at, :] = (re * k_re - im * k_im).astype(BF16)
        src[low, :] = (re * k_im + im * k_re).astype(BF16)

    def keep(i, at, low, re, im):
        psi[0, at, :] = re
        psi[1, at, :] = im

    transform(src, fwd, bwd, mid, propagate)
    transform(src, bwd, fwd, mid, keep)


def second_kernel(
    rows_ref, count_ref, top, body, bottom, psi, amp, cos, sin, grad, back, window, fwd, bwd, src, mid
):
    n = cos.shape[0]
    make_tables(cos, sin, fwd, bwd)
    load_window(top, body, bottom, window)
    start = rows_ref[0]
    weight = jnp.where(count_ref[0] > 0, 1.0, 0.0).astype(F32)
    grad[...] = jnp.zeros_like(grad)

    @pl.loop(0, n // H)
    def _(i):
        at = pl.ds(pl.multiple_of(i * H, H), H)
        low = pl.ds(pl.multiple_of(n + i * H, H), H)
        b_re = take_rows(window, 0, start, i * H, H)
        b_im = take_rows(window, 1, start, i * H, H)
        p_re, p_im = psi[0, at, :], psi[1, at, :]
        src[at, :] = (p_re * b_re - p_im * b_im).astype(BF16)
        src[low, :] = (p_re * b_im + p_im * b_re).astype(BF16)

    def detect(i, at, low, re, im):
        factor = 1.0 - amp[at, :].astype(F32) / jnp.sqrt(re * re + im * im + 1.0)
        src[at, :] = (re * factor).astype(BF16)
        src[low, :] = (im * factor).astype(BF16)

    def spread(i, at, low, re, im):
        p_re, p_im = psi[0, at, :], psi[1, at, :]
        b_re = take_rows(window, 0, start, i * ROWS, ROWS)
        b_im = take_rows(window, 1, start, i * ROWS, ROWS)
        add_rows(grad, 0, start, i * ROWS, weight * (p_re * re + p_im * im))
        add_rows(grad, 1, start, i * ROWS, weight * (p_re * im - p_im * re))
        back[at, :] = (b_re * re + b_im * im).astype(BF16)
        back[low, :] = (b_re * im - b_im * re).astype(BF16)

    transform(src, fwd, bwd, mid, detect)
    transform(src, bwd, fwd, mid, spread)


def third_kernel(rows_ref, count_ref, back, probe, k, cos, sin, grad, fwd, bwd, src, mid):
    make_tables(cos, sin, fwd, bwd)
    start = rows_ref[0]
    weight = jnp.where(count_ref[0] > 0, 1.0, 0.0).astype(F32)
    grad[...] = jnp.zeros_like(grad)

    def propagate(i, at, low, re, im):
        k_re, k_im = k[0, at, :], k[1, at, :]
        src[at, :] = (re * k_re + im * k_im).astype(BF16)
        src[low, :] = (im * k_re - re * k_im).astype(BF16)

    def finish(i, at, low, re, im):
        q_re, q_im = probe[0, at, :], probe[1, at, :]
        add_rows(grad, 0, start, i * ROWS, weight * (q_re * re + q_im * im))
        add_rows(grad, 1, start, i * ROWS, weight * (q_re * im - q_im * re))

    transform(back, fwd, bwd, mid, propagate)
    transform(src, bwd, fwd, mid, finish)


def work(n):
    return [
        pltpu.VMEM((2 * n, 2 * n), BF16),
        pltpu.VMEM((2 * n, 2 * n), BF16),
        pltpu.VMEM((2 * n, n), BF16),
        pltpu.VMEM((n, 2 * n), BF16),
    ]


def gather(cols_ref, grad, above, below, wide):
    rows = wide.shape[0]
    width = grad.shape[-1]
    wide[...] = jnp.zeros_like(wide)

    def add(row, block, start):
        base = pl.multiple_of(start // LANES * LANES, LANES)
        block = jnp.concatenate([block, jnp.zeros((H, LANES), F32)], axis=1)
        wide[pl.ds(row, H), pl.ds(base, width + LANES)] += pltpu.roll(block, start % LANES, axis=1)

    @pl.loop(0, rows // H)
    def _(i):
        add(pl.multiple_of(i * H, H), grad[0, pl.ds(pl.multiple_of(H + i * H, H), H), :], cols_ref[0])

    add(0, above[0], cols_ref[1])
    add(rows - H, below[0], cols_ref[2])


def spill_kernel(limit, cols_ref, first, last, *rest):
    edges_near, (to_left, to_right) = rest[:4], rest[4:]
    rows = to_left.shape[1]

    def cut(near, far, start):
        lane = lax.broadcasted_iota(jnp.int32, near.shape, 1)
        turn = start % LANES
        return (
            jnp.where(lane >= start, pltpu.roll(near, turn, axis=1), 0.0),
            jnp.where(lane < start - limit, pltpu.roll(far, turn, axis=1), 0.0),
        )

    to_left[0], to_right[0] = cut(first[0, H : H + rows, :], last[0, H : H + rows, :], cols_ref[0])
    for near, far, at, which in (edges_near[:2] + (0, 1), edges_near[2:] + (rows - H, 2)):
        left, right = cut(near[0], far[0], cols_ref[which])
        to_left[0, at : at + H, :] += left
        to_right[0, at : at + H, :] += right


def place_kernel(s, cols_ref, step_ref, grad, above, below, left, right, tile, *rest):
    out, wide = rest[-2:]
    inner = tile.shape[-1]
    gather(cols_ref, grad, above, below, wide)
    wide[:, H : 2 * H] += left[0]
    wide[:, inner : H + inner] += right[0]
    out[0, 0] = tile[0, 0] - step_ref[s] * wide[:, H : H + inner]


def gradient_specs(grad, rows):
    edge = pl.BlockSpec((1, H, grad.shape[-1]), lambda c: (c, 0, 0))
    side = pl.BlockSpec((1, rows, H), lambda c: (c, 0, 0))
    return [pl.BlockSpec((1,) + grad.shape[1:], lambda c: (c, 0, 0)), edge, edge], [side, side]


def spill(cols, grad, above, below, tile):
    rows, inner = tile.shape[2:]
    width = grad.shape[-1]
    final = width // H - 1
    ends = lambda array: [
        pl.BlockSpec((1, array.shape[1], H), lambda c, e=e: (c, 0, e)) for e in (0, final)
    ]
    return pl.pallas_call(
        functools.partial(spill_kernel, inner + H - width),
        grid=(2,),
        in_specs=[SMEM] + ends(grad) + ends(above) + ends(below),
        out_specs=[pl.BlockSpec((1, rows, H), lambda c: (c, 0, 0))] * 2,
        out_shape=[jax.ShapeDtypeStruct((2, rows, H), F32)] * 2,
        **params(0, 4 << 20),
    )(cols, grad, grad, above, above, below, below)


def place(cols, step, grad, above, below, left, right, tile, s, so_far):
    rows, inner = tile.shape[2:]
    sources, sides = gradient_specs(grad, rows)
    plane = pl.BlockSpec((1, 1, rows, inner), lambda c: (s, c, 0, 0))
    more = [] if so_far is None else [so_far]
    return pl.pallas_call(
        functools.partial(place_kernel, s),
        grid=(2,),
        in_specs=[SMEM, SMEM] + sources + sides + [plane] + [pl.BlockSpec(memory_space=pl.ANY)] * len(more),
        out_specs=plane,
        out_shape=jax.ShapeDtypeStruct(tile.shape, F32),
        scratch_shapes=[pltpu.VMEM((rows, inner + 2 * H + LANES), F32)],
        input_output_aliases={8: 0} if more else {},
        **params(0, 14 << 20),
    )(cols, step, grad, above, below, left, right, tile, *more)


def per_device(object_tiles, probe, prop_phase, amplitudes, offsets, counts, step_size):
    n = probe.shape[1]
    rows, inner = object_tiles.shape[2:]
    cos, sin = dft_table(n)
    kernel = jnp.stack([jnp.cos(prop_phase), jnp.sin(prop_phase)])
    mine = offsets[0, 0, 0]
    above = shifted(mine, "rows", 1)
    below = shifted(mine, "rows", -1)
    cols = jnp.stack([mine[1], above[1], below[1]])
    row = mine[:1]
    count = counts[0]

    lefts, rights, tops, bottoms = [], [], [], []
    for s in range(2):
        high, low = object_tiles[s, :, :, inner - H :], object_tiles[s, :, :, :H]
        lefts.append(shifted(high, "cols", 1))
        rights.append(shifted(low, "cols", -1))
    for s in range(2):
        up, down = edges(cols, object_tiles, lefts[s], rights[s], s, n)
        tops.append(shifted(down, "rows", 1))
        bottoms.append(shifted(up, "rows", -1))
    bodies = [middle(cols, object_tiles, lefts[s], rights[s], s, n) for s in range(2)]

    per_transform = 2 * 2 * (2 * n) * (2 * n) * n
    ext = jax.ShapeDtypeStruct((2, rows + 2 * H + SUBLANES, n), F32)
    field = jax.ShapeDtypeStruct((2, n, n), F32)
    window = pltpu.VMEM(ext.shape, F32)
    psi = pl.pallas_call(
        first_kernel,
        in_specs=[SMEM] + [VMEM] * 7,
        out_specs=VMEM,
        out_shape=field,
        scratch_shapes=[window] + work(n),
        name="first",
        **params(2 * per_transform, 12 << 20),
    )(row, tops[0], bodies[0], bottoms[0], probe, kernel, cos, sin)
    grad2, back = pl.pallas_call(
        second_kernel,
        in_specs=[SMEM] * 2 + [VMEM] * 7,
        out_specs=[VMEM, VMEM],
        out_shape=[ext, jax.ShapeDtypeStruct((2 * n, n), BF16)],
        scratch_shapes=[window] + work(n),
        name="second",
        **params(2 * per_transform, 14 << 20),
    )(row, count, tops[1], bodies[1], bottoms[1], psi, amplitudes[0, 0, 0], cos, sin)
    grad1 = pl.pallas_call(
        third_kernel,
        in_specs=[SMEM] * 2 + [VMEM] * 5,
        out_specs=VMEM,
        out_shape=ext,
        scratch_shapes=work(n),
        name="third",
        **params(2 * per_transform, 12 << 20),
    )(row, count, back, probe, kernel, cos, sin)

    parts = []
    for s, grad in ((1, grad2), (0, grad1)):
        from_above = shifted(grad[:, rows + H : rows + 2 * H], "rows", 1)
        from_below = shifted(grad[:, :H], "rows", -1)
        to_left, to_right = spill(cols, grad, from_above, from_below, object_tiles)
        from_left, from_right = shifted(to_right, "cols", 1), shifted(to_left, "cols", -1)
        parts.append((s, (grad, from_above, from_below, from_left, from_right)))
    out = None
    for s, pieces in parts:
        out = place(cols, step_size, *pieces, object_tiles, s, out)
    return out


def solution(mesh):
    return jax.shard_map(
        per_device,
        mesh=mesh,
        in_specs=(
            P(None, None, "rows", "cols"),
            P(),
            P(),
            P("rows", "cols", None, None, None),
            P("rows", "cols", None, None),
            P("rows", "cols"),
            P(),
        ),
        out_specs=P(None, None, "rows", "cols"),
        check_vma=False,
    )
```
